256 devices in a mesh: tp: 32 (over z, x_lo, core), dp: 8 (over x_hi, y).
Axes of the slice: x: 4 (x_hi: 2, x_lo: 2; x = x_hi * 2 + x_lo), y: 4, z: 8, core: 2. Of those that a mesh axis runs over, the one named last changes fastest.
Arguments:
- forget_inputs: bfloat16 [4096, 8192], P(('tp', 'dp')), may hold values from -6 to 6
- gate_pre: bfloat16 [4096, 16384], P('dp', 'tp'), may hold values from -6 to 6
- up_pre: bfloat16 [4096, 16384], P('dp', 'tp'), may hold values from -6 to 6
- hidden_grad: bfloat16 [4096, 16384], P('dp', 'tp'), may hold values from -6 to 6
- gate_weight: bfloat16 [8192, 16384], P('dp', 'tp'), may hold values from -0.0625 to 0.0625
- up_weight: bfloat16 [8192, 16384], P('dp', 'tp'), may hold values from -0.0625 to 0.0625
- retain_gate: float32 [8192, 16384], P('dp', 'tp'), may hold values from 0.002 to 0.2
- retain_up: float32 [8192, 16384], P('dp', 'tp'), may hold values from 0.002 to 0.2
Outputs:
- new_gate: bfloat16 [8192, 16384], P('dp', 'tp')
- new_up: bfloat16 [8192, 16384], P('dp', 'tp')
The draws below stay inside these ranges and needn't reach their ends.
All inputs are finite; a program needn't handle non-finite values.
Results may differ from the reference program's by a relative error of at most 0.0064.
Values may be sent and summed in bfloat16 or wider, within the bound.
No kernel may reach another device: no remote copies, remote signals or barrier semaphores. Data moves between devices by JAX's collectives and lax.ppermute only.
A program may use at most 128 MiB of HBM per device.

```python
import math
import jax
import jax.numpy as jnp

D = 8192
FF = 16384
TOKENS = 4096


def shard_levels(rng, shape, pieces, least, high):
    gain, own = 1.0, jax.random.fold_in(rng, 6)
    for position, blocks in pieces:
        heights = jnp.exp(jax.random.uniform(jax.random.fold_in(own, position), (blocks,), jnp.float32, least / len(pieces), high / len(pieces)))
        gain = gain * jnp.repeat(heights, shape[position] // blocks).reshape([-1 if axis == position else 1 for axis in range(len(shape))])
    return gain


def centred(own_key, dims, deviation, bound, split=(), kind=jnp.bfloat16):
    factor_of = shard_levels(own_key, dims, split, -0.22, 0.18) if split else 1.0
    array = jax.random.normal(own_key, dims, jnp.float32) * deviation * factor_of
    return jnp.minimum(jnp.maximum(array, -bound), bound).astype(kind)


def setup_inputs(seed: int = 0) -> dict:
    arg_keys = jax.random.split(jax.random.key(seed), 9)
    return {
        "forget_inputs": centred(arg_keys[0], (TOKENS, D), 1.0, 6.0, ((0, 256),)),
        "gate_pre": centred(arg_keys[1], (TOKENS, FF), 1.5, 6.0, ((0, 8), (1, 32))),
        "up_pre": centred(arg_keys[2], (TOKENS, FF), 1.0, 6.0, ((0, 8), (1, 32))),
        "hidden_grad": centred(arg_keys[3], (TOKENS, FF), 1.0, 6.0, ((0, 8), (1, 32))),
        "gate_weight": centred(arg_keys[4], (D, FF), D ** -0.5, 0.0625, ((0, 8), (1, 32))),
        "up_weight": centred(arg_keys[5], (D, FF), D ** -0.5, 0.0625, ((0, 8), (1, 32))),
        "retain_gate": jnp.clip(jnp.exp(math.log(0.2) - 4.6051702 * jax.random.uniform(arg_keys[6], (D, FF), jnp.float32) ** shard_levels(arg_keys[6], (D, FF), ((0, 8), (1, 32)), -0.2, 0.2)), 0.002, 0.2),
        "retain_up": jnp.clip(jnp.exp(math.log(0.2) - 4.6051702 * jax.random.uniform(arg_keys[7], (D, FF), jnp.float32) ** shard_levels(arg_keys[7], (D, FF), ((0, 8), (1, 32)), -0.2, 0.2)), 0.002, 0.2),
    }


select_ratio = 10.0
dampen_ratio = 10.0


def reference(forget_inputs, gate_pre, up_pre, hidden_grad, gate_weight, up_weight, retain_gate, retain_up):
    gate_val = gate_pre.astype(jnp.float32)
    up_val = up_pre.astype(jnp.float32)
    grad_val = hidden_grad.astype(jnp.float32)
    sig = jax.nn.sigmoid(gate_val)
    gate_delta = (grad_val * up_val * sig * (1.0 + gate_val * (1.0 - sig))).astype(jnp.bfloat16)
    up_delta = (grad_val * gate_val * sig).astype(jnp.bfloat16)
    inputs_wide = forget_inputs.astype(jnp.float32)
    gate_sum = jnp.dot(inputs_wide.T, gate_delta.astype(jnp.float32), preferred_element_type=jnp.float32)
    up_sum = jnp.dot(inputs_wide.T, up_delta.astype(jnp.float32), preferred_element_type=jnp.float32)
    gate_forget = gate_sum * gate_sum / TOKENS
    up_forget = up_sum * up_sum / TOKENS
    gate_factor = dampen_ratio * retain_gate / jnp.maximum(gate_forget, select_ratio * retain_gate)
    up_factor = dampen_ratio * retain_up / jnp.maximum(up_forget, select_ratio * retain_up)
    new_gate = (gate_weight.astype(jnp.float32) * gate_factor).astype(jnp.bfloat16)
    new_up = (up_weight.astype(jnp.float32) * up_factor).astype(jnp.bfloat16)
    return (new_gate, new_up)
```

```python
import jax
import jax.numpy as jnp
from jax import lax
from jax.experimental import pallas as pl
from jax.experimental.pallas import tpu as pltpu
from jax.sharding import PartitionSpec as P

select_ratio = 10.0
dampen_ratio = 10.0


NZ = 8
NY = 4
TP = 32
DP = 8
TILE = 256


def z_shift(step):
    return [(t, ((t // 4 + step) % NZ) * 4 + t % 4) for t in range(TP)]


def y_shift(step):
    return [(d, (d // NY) * NY + (d % NY + step) % NY) for d in range(DP)]


def flip(n, bit):
    return [(i, i ^ bit) for i in range(n)]


def dampened(weight, retain, summed, count):
    forget = summed * summed / count
    factor = dampen_ratio * retain / jnp.maximum(forget, select_ratio * retain)
    return (weight.astype(jnp.float32) * factor).astype(jnp.bfloat16)


def final_kernel(*refs):
    where = refs[0]
    a_refs = refs[1:17]
    b_refs = refs[17:27]
    gw, uw, rg, ru, og, ou, a_mem, b_mem, sem = refs[27:]

    @pl.when(pl.program_id(0) == 0)
    def _():
        copies = []
        for n, ref in enumerate(a_refs):
            copies.append(pltpu.make_async_copy(ref, a_mem.at[where[n]], sem.at[len(copies)]))
        for n, ref in enumerate(b_refs):
            rows = ref.shape[0]
            for r in range(0, rows, 128):
                row = r + (256 if n == 9 or n == 4 else 0)
                x_lo, core = row // 256, (row // 128) % 2
                copies.append(
                    pltpu.make_async_copy(
                        ref.at[pl.ds(r, 128)],
                        b_mem.at[where[16 + n] + core, pl.ds(x_lo * 128, 128)],
                        sem.at[len(copies)],
                    )
                )
        for c in copies:
            c.start()
        for c in copies:
            c.wait()

    start = pl.multiple_of(pl.program_id(0) * TILE, TILE)
    lhs = jnp.concatenate([a_mem[k, pl.ds(start, TILE), :] for k in range(16)], axis=1)
    for half, (w, r, o) in enumerate(((gw, rg, og), (uw, ru, ou))):
        rhs = b_mem[:, :, half * 512 : half * 512 + 512].reshape(4096, 512)
        total = jnp.dot(lhs, rhs, preferred_element_type=jnp.float32)
        o[...] = dampened(w[...], r[...], total, 4096.0)


def finish(where, a_pieces, b_pieces, gw, uw, rg, ru):
    block = pl.BlockSpec((TILE, 512), lambda i: (i, 0))
    hbm = pl.BlockSpec(memory_space=pl.ANY)
    out = jax.ShapeDtypeStruct((1024, 512), jnp.bfloat16)
    return pl.pallas_call(
        final_kernel,
        grid=(1024 // TILE,),
        out_shape=(out, out),
        in_specs=[pl.BlockSpec(memory_space=pltpu.SMEM)]
        + [hbm] * (len(a_pieces) + len(b_pieces))
        + [block] * 4,
        out_specs=(block, block),
        scratch_shapes=[
            pltpu.VMEM((16, 1024, 256), jnp.bfloat16),
            pltpu.VMEM((16, 256, 1024), jnp.bfloat16),
            pltpu.SemaphoreType.DMA((48,)),
        ],
        compiler_params=pltpu.CompilerParams(vmem_limit_bytes=56 << 20),
        name="finish",
    )(where, *a_pieces, *b_pieces, gw, uw, rg, ru)


def body(
    forget_inputs, gate_pre, up_pre, hidden_grad, gate_weight, up_weight, retain_gate, retain_up
):
    tp, dp = lax.axis_index("tp"), lax.axis_index("dp")
    z, x_lo, core = tp // 4, (tp // 2) % 2, tp % 2
    x_hi, y = dp // NY, dp % NY

    gate_val = gate_pre.astype(jnp.float32)
    up_val = up_pre.astype(jnp.float32)
    grad_val = hidden_grad.astype(jnp.float32)
    sig = jax.nn.sigmoid(gate_val)
    gate_delta = (grad_val * up_val * sig * (1.0 + gate_val * (1.0 - sig))).astype(jnp.bfloat16)
    up_delta = (grad_val * gate_val * sig).astype(jnp.bfloat16)
    delta = jnp.concatenate([gate_delta, up_delta], axis=1)

    columns = lax.all_to_all(forget_inputs, "dp", split_axis=1, concat_axis=0, tiled=True)
    other = lax.ppermute(columns, "tp", flip(TP, 2))
    mine = jnp.where(
        x_lo == 0,
        jnp.concatenate([columns, other], axis=0),
        jnp.concatenate([other, columns], axis=0),
    ).T

    across = lax.ppermute(delta, "dp", flip(DP, 4))
    b_pieces, b_where = [], []
    for half, base in ((0, delta), (1, across)):
        below = lax.ppermute(base, "dp", y_shift(1))
        above = lax.ppermute(base, "dp", y_shift(-1))
        far_top = lax.ppermute(below[:256], "dp", y_shift(1))
        far_low = lax.ppermute(above[256:], "dp", y_shift(-1))
        side = (x_hi ^ half) * NY
        b_pieces += [base, below, above, far_top, far_low]
        far = side + (y + 2) % NY
        b_where += [side + y, side + (y + 3) % NY, side + (y + 1) % NY, far, far]

    ring = {0: mine}
    up, down = mine, mine
    for step in range(1, 4):
        up = lax.ppermute(up, "tp", z_shift(1))
        down = lax.ppermute(down, "tp", z_shift(-1))
        ring[-step], ring[step] = up, down
    ring[4] = lax.ppermute(up, "tp", z_shift(1))
    a_pieces, a_where = [], []
    for step, piece in ring.items():
        at = ((z + step) % NZ) * 2
        a_pieces += [piece, lax.ppermute(piece, "tp", flip(TP, 1))]
        a_where += [at + core, at + 1 - core]

    where = jnp.stack([w.astype(jnp.int32) for w in a_where + [2 * w for w in b_where]])
    return finish(where, a_pieces, b_pieces, gate_weight, up_weight, retain_gate, retain_up)


def solution(mesh):
    placed = (P(("tp", "dp"), None),) + (P("dp", "tp"),) * 7
    return jax.shard_map(
        body, mesh=mesh, in_specs=placed, out_specs=(P("dp", "tp"), P("dp", "tp")), check_vma=False
    )
```

```python
import functools

import jax
import jax.numpy as jnp
from jax import lax
from jax.experimental import pallas as pl
from jax.experimental.pallas import tpu as pltpu
from jax.sharding import PartitionSpec as P

select_ratio = 10.0
dampen_ratio = 10.0


NZ = 8
NY = 4
TP = 32
DP = 8
TILE = 256


def z_shift(step):
    return [(t, ((t // 4 + step) % NZ) * 4 + t % 4) for t in range(TP)]


def y_shift(step):
    return [(d, (d // NY) * NY + (d % NY + step) % NY) for d in range(DP)]


def flip(n, bit):
    return [(i, i ^ bit) for i in range(n)]


def dampened(weight, retain, summed, count):
    forget = summed * summed / count
    factor = dampen_ratio * retain / jnp.maximum(forget, select_ratio * retain)
    return (weight.astype(jnp.float32) * factor).astype(jnp.bfloat16)


def delta_kernel(g_ref, u_ref, h_ref, o_ref):
    gate_val = g_ref[...].astype(jnp.float32)
    up_val = u_ref[...].astype(jnp.float32)
    grad_val = h_ref[...].astype(jnp.float32)
    sig = jax.nn.sigmoid(gate_val)
    gate_delta = grad_val * up_val * sig * (1.0 + gate_val * (1.0 - sig))
    o_ref[:, :512] = gate_delta.astype(jnp.bfloat16)
    o_ref[:, 512:] = (grad_val * gate_val * sig).astype(jnp.bfloat16)


def deltas(gate_pre, up_pre, hidden_grad, half):
    block = pl.BlockSpec((128, 512), lambda i: (i + 2 * half, 0))
    return pl.pallas_call(
        delta_kernel,
        grid=(2,),
        out_shape=jax.ShapeDtypeStruct((256, 1024), jnp.bfloat16),
        in_specs=[block] * 3,
        out_specs=pl.BlockSpec((128, 1024), lambda i: (i, 0)),
        name="deltas",
    )(gate_pre, up_pre, hidden_grad)


def split_kernel(me, x_ref, *o_refs):
    for k, o in enumerate(o_refs):
        column = pl.multiple_of(lax.rem(me[0] + k, DP) * 1024, 1024)
        o[...] = x_ref[:, pl.ds(column, 1024)]


def join_kernel(me, *refs):
    for k, r in enumerate(refs[:-1]):
        row = pl.multiple_of(lax.rem(me[0] + DP - k, DP) * 16, 16)
        refs[-1][pl.ds(row, 16), :] = r[...]


def exchange(forget_inputs, me, ahead):
    smem, vmem = pl.BlockSpec(memory_space=pltpu.SMEM), pl.BlockSpec(memory_space=pltpu.VMEM)
    part = jax.ShapeDtypeStruct((16, 1024), jnp.bfloat16)
    parts = pl.pallas_call(
        split_kernel,
        out_shape=[part] * DP,
        in_specs=[smem, vmem],
        out_specs=[vmem] * DP,
        name="split",
    )(me, forget_inputs)
    got = [parts[0]]
    for k in range(1, DP):
        got.append(lax.ppermute(parts[k], "dp", [(d, (d + k) % DP) for d in range(DP)]))
    got, _ = lax.optimization_barrier((got, ahead))
    return pl.pallas_call(
        join_kernel,
        out_shape=jax.ShapeDtypeStruct((128, 1024), jnp.bfloat16),
        in_specs=[smem] + [vmem] * DP,
        out_specs=vmem,
        name="join",
    )(me, *got)


def final_kernel(layout, *refs):
    where = refs[0]
    na, nb = len(layout[0]), len(layout[1])
    a_refs = refs[1 : 1 + na]
    b_refs = refs[1 + na : 1 + na + nb]
    gw, uw, rg, ru, og, ou, a_mem, b_mem, acc, sem_a, sem_b = refs[1 + na + nb :]
    step = pl.program_id(0)

    @pl.when(step == 0)
    def _():
        for n, ref in enumerate(a_refs):
            slot, row = where[n], layout[0][n]
            pltpu.make_async_copy(
                ref, a_mem.at[slot, pl.ds(row, ref.shape[0])], sem_a.at[slot]
            ).start()
        for n, ref in enumerate(b_refs):
            x_lo = layout[1][n]
            for core in range(2):
                slot = where[na + n] + core
                pltpu.make_async_copy(
                    ref.at[pl.ds(core * 128, 128)],
                    b_mem.at[slot, pl.ds(x_lo * 128, 128)],
                    sem_b.at[slot],
                ).start()

    @pl.when(step < 4)
    def _():
        for k in range(4):
            slot = step * 4 + k
            pltpu.make_async_copy(a_mem.at[slot], a_mem.at[slot], sem_a.at[slot]).wait()
            pltpu.make_async_copy(b_mem.at[slot], b_mem.at[slot], sem_b.at[slot]).wait()

    def product(chunk, start, half):
        lhs = jnp.concatenate(
            [a_mem[chunk * 4 + k, pl.ds(start, TILE), :] for k in range(4)], axis=1
        )
        rhs = b_mem[pl.ds(chunk * 4, 4), :, half * 512 : half * 512 + 512].reshape(1024, 512)
        return jnp.dot(lhs, rhs, preferred_element_type=jnp.float32)

    @pl.when(step == 0)
    def _():
        @pl.loop(0, 4)
        def _(m):
            start = pl.multiple_of(m * TILE, TILE)
            for half in range(2):
                acc[half, pl.ds(start, TILE), :] = product(0, start, half)

    @pl.when((step > 0) & (step < 3))
    def _():
        @pl.loop(0, 4)
        def _(m):
            start = pl.multiple_of(m * TILE, TILE)
            for half in range(2):
                acc[half, pl.ds(start, TILE), :] += product(step, start, half)

    @pl.when(step >= 3)
    def _():
        start = pl.multiple_of((step - 3) * TILE, TILE)
        for half, (w, r, o) in enumerate(((gw, rg, og), (uw, ru, ou))):
            total = acc[half, pl.ds(start, TILE), :] + product(3, start, half)
            o[...] = dampened(w[...], r[...], total, 4096.0)


def finish(where, layout, a_pieces, b_pieces, gw, uw, rg, ru):
    block = pl.BlockSpec((TILE, 512), lambda i: (jnp.maximum(i - 3, 0), 0))
    hbm = pl.BlockSpec(memory_space=pl.ANY)
    out = jax.ShapeDtypeStruct((1024, 512), jnp.bfloat16)
    return pl.pallas_call(
        functools.partial(final_kernel, layout),
        grid=(7,),
        out_shape=(out, out),
        in_specs=[pl.BlockSpec(memory_space=pltpu.SMEM)]
        + [hbm] * (len(a_pieces) + len(b_pieces))
        + [block] * 4,
        out_specs=(block, block),
        scratch_shapes=[
            pltpu.VMEM((16, 1024, 256), jnp.bfloat16),
            pltpu.VMEM((16, 256, 1024), jnp.bfloat16),
            pltpu.VMEM((2, 1024, 512), jnp.float32),
            pltpu.SemaphoreType.DMA((16,)),
            pltpu.SemaphoreType.DMA((16,)),
        ],
        compiler_params=pltpu.CompilerParams(vmem_limit_bytes=40 << 20),
        name="finish",
    )(where, *a_pieces, *b_pieces, gw, uw, rg, ru)


def body(
    forget_inputs, gate_pre, up_pre, hidden_grad, gate_weight, up_weight, retain_gate, retain_up
):
    tp, dp = lax.axis_index("tp"), lax.axis_index("dp")
    z, x_lo, core = tp // 4, (tp // 2) % 2, tp % 2
    x_hi, y = dp // NY, dp % NY

    own = [deltas(gate_pre, up_pre, hidden_grad, h) for h in range(2)]

    columns = exchange(forget_inputs, dp.astype(jnp.int32).reshape(1), own)
    other = lax.ppermute(columns, "tp", flip(TP, 2))
    mine = jnp.where(
        x_lo == 0,
        jnp.concatenate([columns, other], axis=0),
        jnp.concatenate([other, columns], axis=0),
    ).T

    b_pieces, b_where, b_half = [], [], []

    def keep(piece, x_side, dy, h):
        b_pieces.append(piece)
        b_where.append(((x_hi ^ x_side) * NY + (y + dy) % NY) * 2)
        b_half.append(h)

    turn = (1, -1)
    across = [lax.ppermute(own[h], "dp", flip(DP, 4)) for h in range(2)]
    for x_side, base in enumerate((own, across)):
        near = {}
        for h in range(2):
            keep(base[h], x_side, 0, h)
            for way in (turn[h], -turn[h]):
                near[h, way] = lax.ppermute(base[h], "dp", y_shift(way))
                keep(near[h, way], x_side, -way, h)
        if x_side == 0:
            for h in range(2):
                far = lax.ppermute(near[h, turn[h]], "dp", y_shift(turn[h]))
                keep(far, 0, 2, h)
                keep(lax.ppermute(far, "dp", flip(DP, 4)), 1, 2, h)

    a_pieces, a_where, a_row = [], [], []

    def place(piece, dz, row):
        at = ((z + dz) % NZ) * 2
        a_pieces.extend([piece, lax.ppermute(piece, "tp", flip(TP, 1))])
        a_where.extend([at + core, at + 1 - core])
        a_row.extend([row, row])

    place(mine, 0, 0)
    up, down = mine, mine
    for step in range(1, 4):
        up = lax.ppermute(up, "tp", z_shift(1))
        down = lax.ppermute(down, "tp", z_shift(-1))
        place(up, -step, 0)
        place(down, step, 0)
    place(lax.ppermute(up[:512], "tp", z_shift(1)), 4, 0)
    place(lax.ppermute(down[512:], "tp", z_shift(-1)), 4, 512)

    where = jnp.stack([w.astype(jnp.int32) for w in a_where + b_where])
    layout = (tuple(a_row), tuple(b_half))
    return finish(
        where, layout, a_pieces, b_pieces, gate_weight, up_weight, retain_gate, retain_up
    )


def solution(mesh):
    placed = (P(("tp", "dp"), None),) + (P("dp", "tp"),) * 7
    return jax.shard_map(
        body, mesh=mesh, in_specs=placed, out_specs=(P("dp", "tp"), P("dp", "tp")), check_vma=False
    )
```
